32 devices in a mesh: sector: 16 (over z, y, x), dof: 2 (over core).
Axes of the slice: x: 2, y: 2, z: 4, core: 2. Of those that a mesh axis runs over, the one named last changes fastest.
Arguments:
- loads: bfloat16 [16, 128, 32768], P('sector', None, 'dof'), may hold values from -0.75 to 0.75
- modes: bfloat16 [32768, 512], P('dof'), may hold values from -0.25 to 0.25
- response: float32 [16, 128, 512], P('sector', None, 'dof'), may hold values from -6 to 6
- pattern: int32 [16], P('sector'), may hold values from 0 to 7
- deviation: float32 [8, 512], replicated, may hold values from -1 to 1
- eigen: float32 [16, 512], replicated, may hold values from 1 to 10
- loss: float32 [512], replicated, may hold values from 0.2 to 0.6
- omega_sq: float32 [64], replicated, may hold values from 0.5 to 12
- iface_left: int32 [1024], P('dof'), may hold values from 0 to 16383, as said below
- iface_right: int32 [1024], P('dof'), may hold values from 0 to 16383, as said below
Outputs:
- modal_response: float32 [16, 128, 512], P('sector', None, 'dof')
- displacement: bfloat16 [16, 128, 32768], P('sector', None, 'dof')
The draws below stay inside these ranges and needn't reach their ends.
Inputs may be any that keep to these rules, and one draw needn't show every extreme that they name: Within each block of 512 entries, the entries of iface_left and of iface_right together are (2) * 512 distinct rows. `iface_right`: see iface_left.
All inputs are finite; a program needn't handle non-finite values.
Results may differ from the reference program's by a relative error of at most 0.005.
Values may be sent and summed in bfloat16 or wider, within the bound.
A program may use at most 128 MiB of HBM per device.

```python
import math
import jax
import jax.numpy as jnp
from jax import lax

M = 512
DOF_DEV = 16384
FREQ = 64
IFC_DEV = 512
PATTERNS = 8
SECTORS = 16
DOFS = 32768
IFACE = 1024
N_DOF = 2


def iface_pick(key):
    base = jax.random.fold_in(key, 7)

    def block(number):
        order = jax.random.permutation(jax.random.fold_in(base, number), DOF_DEV)
        return order[:2 * IFC_DEV]
    return jax.vmap(block)(jnp.arange(N_DOF, dtype=jnp.int32))


def draw_iface_left(key, part):
    return iface_pick(key)[:, :IFC_DEV].reshape(-1).astype(jnp.int32)


def draw_iface_right(key, part):
    return iface_pick(key)[:, IFC_DEV:].reshape(-1).astype(jnp.int32)


def set_ends(values, stream_key, least, high):
    extent = values.shape
    index_at = [jax.random.randint(jax.random.fold_in(stream_key, axis), (), 0, extent[axis]) for axis in range(len(extent))]
    values = values.at[tuple(index_at)].set(least)
    longest = extent.index(max(extent))
    index_at[longest] = (index_at[longest] + 1) % extent[longest]
    return values.at[tuple(index_at)].set(high)


def block_levels(rng, extent, split, low, top_value):
    def one(position, blocks):
        heights = jax.random.uniform(jax.random.fold_in(jax.random.fold_in(rng, 6), position), (blocks,), jnp.float32, low / len(split), top_value / len(split))
        return jnp.repeat(jnp.exp(heights), extent[position] // blocks).reshape((-1,) + (1,) * (len(extent) - position - 1))

    gain = one(*split[0])
    for cut in split[1:]:
        gain = gain * one(*cut)
    return gain


def centred(rng, extent, scale, most, split=(), held_as=jnp.bfloat16):
    factor_of = block_levels(rng, extent, split, -0.22, 0.18) if split else 1.0
    result = jax.random.normal(rng, extent, jnp.float32) * scale * factor_of
    return jnp.minimum(jnp.maximum(result, -most), most).astype(held_as)


def setup_inputs(seed: int = 0) -> dict:
    keys = jax.random.split(jax.random.key(seed), 11)
    return {
        "loads": centred(keys[0], (SECTORS, 2 * FREQ, DOFS), (DOFS // M) ** -0.5, 0.75, ((0, 16), (2, 2))),
        "modes": centred(keys[1], (DOFS, M), M ** -0.5, 0.25, ((0, 2),)),
        "response": centred(keys[2], (SECTORS, 2 * FREQ, M), 1.0, 6.0, ((0, 16), (2, 2)), jnp.float32),
        "pattern": set_ends(jax.random.randint(keys[3], (SECTORS,), 0, PATTERNS), jax.random.fold_in(keys[3], 1), 0, PATTERNS - 1).astype(jnp.int32),
        "deviation": jnp.clip(jax.random.uniform(keys[4], (PATTERNS, M), jnp.float32, -1.0, 1.0), -1.0, 1.0),
        "eigen": jnp.clip(jnp.exp(jax.random.uniform(keys[5], (SECTORS, M), jnp.float32, math.log(1.0), math.log(10.0))), 1.0, 10.0),
        "loss": jnp.clip(jnp.exp(jax.random.uniform(keys[6], (M,), jnp.float32, math.log(0.2), math.log(0.6))), 0.2, 0.6),
        "omega_sq": jnp.clip(jax.random.uniform(keys[7], (FREQ,), jnp.float32, 0.5, 12.0), 0.5, 12.0),
        "iface_left": draw_iface_left(jax.random.fold_in(keys[10], 71), 0),
        "iface_right": draw_iface_right(jax.random.fold_in(keys[10], 71), 0),
    }


def reference(loads, modes, response, pattern, deviation, eigen, loss, omega_sq, iface_left, iface_right):
    hp = lax.Precision.HIGHEST
    force = jnp.dot(loads.reshape(SECTORS * 2 * FREQ, DOFS), modes, preferred_element_type=jnp.float32)
    force = force.reshape(SECTORS, 2, FREQ, M)
    dev_rows = deviation[pattern]
    rest = force - dev_rows[:, None, None, :] * response.reshape(SECTORS, 2, FREQ, M)
    index = jnp.arange(SECTORS, dtype=jnp.int32)
    turns = (index[:, None] * index[None, :]) % SECTORS
    theta = turns.astype(jnp.float32) * (2.0 * math.pi / SECTORS)
    cosine = jnp.cos(theta)
    sine = jnp.sin(theta)
    real_part = rest[:, 0].reshape(SECTORS, FREQ * M)
    imag_part = rest[:, 1].reshape(SECTORS, FREQ * M)
    spec_re = jnp.dot(cosine, real_part, precision=hp) + jnp.dot(sine, imag_part, precision=hp)
    spec_im = jnp.dot(cosine, imag_part, precision=hp) - jnp.dot(sine, real_part, precision=hp)
    spec_re = spec_re.reshape(SECTORS, FREQ, M)
    spec_im = spec_im.reshape(SECTORS, FREQ, M)
    shifted = eigen[:, None, :] - omega_sq[None, :, None]
    damped = loss[None, None, :] * eigen[:, None, :]
    denom = shifted * shifted + damped * damped
    solved_re = ((spec_re * shifted + spec_im * damped) / denom).reshape(SECTORS, FREQ * M)
    solved_im = ((spec_im * shifted - spec_re * damped) / denom).reshape(SECTORS, FREQ * M)
    out_re = (jnp.dot(cosine, solved_re, precision=hp) - jnp.dot(sine, solved_im, precision=hp)) / SECTORS
    out_im = (jnp.dot(cosine, solved_im, precision=hp) + jnp.dot(sine, solved_re, precision=hp)) / SECTORS
    modal_response = jnp.stack([out_re, out_im], 1).reshape(SECTORS, 2 * FREQ, M)
    rounded = modal_response.astype(jnp.bfloat16)
    raw = jnp.dot(rounded.reshape(SECTORS * 2 * FREQ, M), modes.T, preferred_element_type=jnp.float32)
    raw = raw.reshape(SECTORS, 2 * FREQ, DOFS).astype(jnp.bfloat16)
    offsets = (jnp.arange(IFACE, dtype=jnp.int32) // IFC_DEV) * DOF_DEV
    left_rows = (iface_left + offsets).astype(jnp.int32)
    right_rows = (iface_right + offsets).astype(jnp.int32)
    left_vals = raw[:, :, left_rows].astype(jnp.float32)
    right_vals = raw[:, :, right_rows].astype(jnp.float32)
    right_new = (0.5 * (right_vals + jnp.roll(left_vals, -1, axis=0))).astype(jnp.bfloat16)
    left_new = (0.5 * (jnp.roll(right_vals, 1, axis=0) + left_vals)).astype(jnp.bfloat16)
    displacement = raw.at[:, :, right_rows].set(right_new).at[:, :, left_rows].set(left_new)
    return modal_response, displacement
```

```python
import functools
import math

import jax
import jax.numpy as jnp
from jax import lax
from jax.experimental import pallas as pl
from jax.experimental.pallas import tpu as pltpu
from jax.sharding import PartitionSpec as P

MESH = pl.DeviceIdType.MESH
LANES = 128


def shifted_2(shard, axis, by):
    size = lax.axis_size(axis)
    return lax.ppermute(shard, axis, [(i, (i + by) % size) for i in range(size)])


def transform(re, im, sign):
    n = len(re)
    if n == 1:
        return re, im
    if n % 2:
        out_re, out_im = [], []
        for h in range(n):
            sum_re, sum_im = re[0], im[0]
            for s in range(1, n):
                turn = 2.0 * math.pi * ((h * s) % n) / n
                cosine, sine = math.cos(turn), sign * math.sin(turn)
                sum_re = sum_re + re[s] * cosine - im[s] * sine
                sum_im = sum_im + im[s] * cosine + re[s] * sine
            out_re.append(sum_re)
            out_im.append(sum_im)
        return out_re, out_im
    even_re, even_im = transform(re[0::2], im[0::2], sign)
    odd_re, odd_im = transform(re[1::2], im[1::2], sign)
    half = n // 2
    out_re, out_im = [None] * n, [None] * n
    for k in range(half):
        if k == 0:
            turned_re, turned_im = odd_re[k], odd_im[k]
        elif 4 * k == n:
            turned_re, turned_im = -sign * odd_im[k], sign * odd_re[k]
        else:
            cosine = math.cos(2.0 * math.pi * k / n)
            sine = sign * math.sin(2.0 * math.pi * k / n)
            turned_re = odd_re[k] * cosine - odd_im[k] * sine
            turned_im = odd_re[k] * sine + odd_im[k] * cosine
        out_re[k], out_im[k] = even_re[k] + turned_re, even_im[k] + turned_im
        out_re[k + half] = even_re[k] - turned_re
        out_im[k + half] = even_im[k] - turned_im
    return out_re, out_im


def modal_kernel(
    nsec, ndof, steps,
    loads_ref, modes_ref, resp_ref, pattern_ref, dev_ref, eigen_ref, loss_ref, omega_ref,
    mine_ref, full_ref,
    acc, send_a, recv_a, send_b, recv_b, coef, sa, ra, sb, rb,
):
    step = pl.program_id(0)
    sec, dof = lax.axis_index("sector"), lax.axis_index("dof")
    count = nsec * ndof
    me = sec * ndof + dof
    rows, modes_all = acc.shape
    freqs, half = rows // 2, modes_all // ndof
    groups, share = half // LANES, freqs // nsec
    part = groups * share
    barrier = pltpu.get_barrier_semaphore()

    def peer(k):
        return lax.rem(me + k, count)

    def place(device):
        return {"sector": device // ndof, "dof": lax.rem(device, ndof)}

    @pl.when(step == 0)
    def _():
        acc[...] = jnp.zeros_like(acc)

        def greet(k, carry):
            pl.semaphore_signal(barrier, inc=1, device_id=place(peer(k)), device_id_type=MESH)
            return carry

        lax.fori_loop(1, count, greet, 0)

    acc[...] += jnp.dot(loads_ref[...], modes_ref[...], preferred_element_type=jnp.float32)

    def pick(values):
        total = None
        for d in range(ndof):
            term = jnp.where(dof == d, values[:, d * half : (d + 1) * half], 0.0)
            total = term if total is None else total + term
        return total

    def pieces():
        for kind in range(2):
            for g in range(groups):
                yield kind, g, (kind * groups + g) * share

    @pl.when(step == steps - 1)
    def _():
        table = dev_ref[...]
        chosen = lax.broadcasted_iota(jnp.int32, table.shape, 0) == pattern_ref[0]
        dev_row = pick(jnp.sum(jnp.where(chosen, table, 0.0), axis=0, keepdims=True))
        scaled = dev_row * resp_ref[...]
        for d in range(ndof):
            cols = slice(d * half, (d + 1) * half)
            acc[:, cols] = acc[:, cols] - jnp.where(dof == d, scaled, 0.0)
        for t in range(nsec):
            for d in range(ndof):
                parts = []
                for kind, g, _ in pieces():
                    first = kind * freqs + t * share
                    left = d * half + g * LANES
                    parts.append(acc[first : first + share, left : left + LANES])
                send_a[t * ndof + d] = jnp.concatenate(parts, 0).astype(jnp.bfloat16)
        pl.semaphore_wait(barrier, count - 1)

        def copy_a(to, origin):
            return pltpu.make_async_remote_copy(
                src_ref=send_a.at[to], dst_ref=recv_a.at[origin],
                send_sem=sa.at[to], recv_sem=ra.at[origin],
                device_id=place(to), device_id_type=MESH,
            )

        def copy_b(to, origin):
            return pltpu.make_async_remote_copy(
                src_ref=send_b.at[to // ndof], dst_ref=recv_b.at[origin],
                send_sem=sb.at[to], recv_sem=rb.at[origin],
                device_id=place(to), device_id_type=MESH,
            )

        def start_a(k, carry):
            copy_a(peer(k), me).start()
            return carry

        lax.fori_loop(1, count, start_a, 0)
        recv_a[pl.ds(me, 1)] = send_a[pl.ds(me, 1)]

        row = lax.rem(lax.broadcasted_iota(jnp.int32, (part, LANES), 0), share)
        omega = jnp.zeros((part, LANES), jnp.float32)
        for j in range(share):
            omega = jnp.where(row == j, omega_ref[sec * share + j], omega)

        def spread(line):
            line = pick(line)
            return jnp.concatenate(
                [
                    jnp.broadcast_to(line[:, g * LANES : (g + 1) * LANES], (share, LANES))
                    for g in range(groups)
                ],
                0,
            )

        loss = spread(loss_ref[...])
        for h in range(nsec):
            stiff = spread(eigen_ref[h : h + 1, :])
            shifted, damped = stiff - omega, loss * stiff
            denom = shifted * shifted + damped * damped
            coef[0, h] = shifted / denom
            coef[1, h] = damped / denom

        def wait_a(k, carry):
            copy_a(peer(k), peer(k)).wait_recv()
            return carry

        lax.fori_loop(1, count, wait_a, 0)
        rest_re, rest_im = [], []
        for s in range(nsec):
            block = recv_a[s * ndof].astype(jnp.float32)
            for d in range(1, ndof):
                block = block + recv_a[s * ndof + d].astype(jnp.float32)
            rest_re.append(block[:part])
            rest_im.append(block[part:])
        spec_re, spec_im = transform(rest_re, rest_im, -1.0)
        solved_re, solved_im = [], []
        for h in range(nsec):
            a, b = coef[0, h], coef[1, h]
            solved_re.append(spec_re[h] * a + spec_im[h] * b)
            solved_im.append(spec_im[h] * a - spec_re[h] * b)
        out_re, out_im = transform(solved_re, solved_im, 1.0)
        for s in range(nsec):
            block = jnp.concatenate([out_re[s], out_im[s]], 0) * (1.0 / nsec)
            send_b[s] = block.astype(jnp.bfloat16)

        def start_b(k, carry):
            copy_b(peer(k), me).start()
            return carry

        lax.fori_loop(1, count, start_b, 0)
        recv_b[pl.ds(me, 1)] = send_b[pl.ds(sec, 1)]

        def wait_b(k, carry):
            copy_b(peer(k), peer(k)).wait_recv()
            return carry

        lax.fori_loop(1, count, wait_b, 0)
        for t in range(nsec):
            for d in range(ndof):
                block = recv_b[t * ndof + d].astype(jnp.float32)
                for kind, g, at in pieces():
                    first = kind * freqs + t * share
                    left = d * half + g * LANES
                    acc[first : first + share, left : left + LANES] = block[at : at + share]
        whole = acc[...]
        full_ref[...] = whole.astype(jnp.bfloat16)
        mine_ref[...] = pick(whole)

        def sent(k, carry):
            copy_a(peer(k), me).wait_send()
            copy_b(peer(k), me).wait_send()
            return carry

        lax.fori_loop(1, count, sent, 0)


def modal_solve(loads, modes, response, pattern, deviation, eigen, loss, omega_sq):
    rows, depth = loads.shape
    modes_all = modes.shape[1]
    nsec, ndof = lax.axis_size("sector"), lax.axis_size("dof")
    half = modes_all // ndof
    count = nsec * ndof
    part = (half // LANES) * (rows // 2 // nsec)
    tile = min(depth, 2048)
    steps = depth // tile

    def still(shape):
        return pl.BlockSpec(shape, lambda k: (0,) * len(shape))

    smem = pl.BlockSpec(memory_space=pltpu.SMEM)
    block = (2 * part, LANES)
    return pl.pallas_call(
        functools.partial(modal_kernel, nsec, ndof, steps),
        grid=(steps,),
        out_shape=(
            jax.ShapeDtypeStruct((rows, half), jnp.float32),
            jax.ShapeDtypeStruct((rows, modes_all), jnp.bfloat16),
        ),
        in_specs=[
            pl.BlockSpec((rows, tile), lambda k: (0, k)),
            pl.BlockSpec((tile, modes_all), lambda k: (k, 0)),
            still(response.shape),
            smem,
            still(deviation.shape),
            still(eigen.shape),
            still((1, modes_all)),
            smem,
        ],
        out_specs=(still((rows, half)), still((rows, modes_all))),
        scratch_shapes=[
            pltpu.VMEM((rows, modes_all), jnp.float32),
            pltpu.VMEM((count,) + block, jnp.bfloat16),
            pltpu.VMEM((count,) + block, jnp.bfloat16),
            pltpu.VMEM((nsec,) + block, jnp.bfloat16),
            pltpu.VMEM((count,) + block, jnp.bfloat16),
            pltpu.VMEM((2, nsec, part, LANES), jnp.float32),
            pltpu.SemaphoreType.DMA((count,)),
            pltpu.SemaphoreType.DMA((count,)),
            pltpu.SemaphoreType.DMA((count,)),
            pltpu.SemaphoreType.DMA((count,)),
        ],
        compiler_params=pltpu.CompilerParams(
            dimension_semantics=("arbitrary",), collective_id=0, has_side_effects=True
        ),
        name="modal_solve",
    )(loads, modes, response, pattern, deviation, eigen, loss.reshape(1, modes_all), omega_sq)


def shards(
    loads, modes, response, pattern, deviation, eigen, loss, omega_sq, iface_left, iface_right
):
    mine, full = modal_solve(
        loads[0], modes, response[0], pattern, deviation, eigen, loss, omega_sq
    )
    modal_response = mine[None]
    raw = jnp.einsum(
        "skm,dm->skd", full[None], modes, preferred_element_type=jnp.float32
    ).astype(jnp.bfloat16)
    left_vals = jnp.take(raw, iface_left, axis=2)
    right_vals = jnp.take(raw, iface_right, axis=2)
    next_left = shifted_2(left_vals, "sector", -1)
    prev_right = shifted_2(right_vals, "sector", 1)
    left_after = next_left
    right_before = prev_right
    right_new = (0.5 * (right_vals.astype(jnp.float32) + left_after.astype(jnp.float32))).astype(
        jnp.bfloat16
    )
    left_new = (0.5 * (right_before.astype(jnp.float32) + left_vals.astype(jnp.float32))).astype(
        jnp.bfloat16
    )
    displacement = raw.at[:, :, iface_right].set(right_new).at[:, :, iface_left].set(left_new)
    return (modal_response, displacement)


def solution(mesh):
    placed = (
        P("sector", None, "dof"),
        P("dof", None),
        P("sector", None, "dof"),
        P("sector"),
        P(),
        P(),
        P(),
        P(),
        P("dof"),
        P("dof"),
    )
    return jax.shard_map(
        shards,
        mesh=mesh,
        in_specs=placed,
        out_specs=(P("sector", None, "dof"), P("sector", None, "dof")),
        check_vma=False,
    )
```

```python
import functools
import math

import jax
import jax.numpy as jnp
from jax import lax
from jax.experimental import pallas as pl
from jax.experimental.pallas import tpu as pltpu
from jax.sharding import PartitionSpec as P

MESH = pl.DeviceIdType.MESH
LANES = 128


def transform(re, im, sign):
    n = len(re)
    if n == 1:
        return re, im
    if n % 2:
        out_re, out_im = [], []
        for h in range(n):
            sum_re, sum_im = re[0], im[0]
            for s in range(1, n):
                turn = 2.0 * math.pi * ((h * s) % n) / n
                cosine, sine = math.cos(turn), sign * math.sin(turn)
                sum_re = sum_re + re[s] * cosine - im[s] * sine
                sum_im = sum_im + im[s] * cosine + re[s] * sine
            out_re.append(sum_re)
            out_im.append(sum_im)
        return out_re, out_im
    even_re, even_im = transform(re[0::2], im[0::2], sign)
    odd_re, odd_im = transform(re[1::2], im[1::2], sign)
    half = n // 2
    out_re, out_im = [None] * n, [None] * n
    for k in range(half):
        if k == 0:
            turned_re, turned_im = odd_re[k], odd_im[k]
        elif 4 * k == n:
            turned_re, turned_im = -sign * odd_im[k], sign * odd_re[k]
        else:
            cosine = math.cos(2.0 * math.pi * k / n)
            sine = sign * math.sin(2.0 * math.pi * k / n)
            turned_re = odd_re[k] * cosine - odd_im[k] * sine
            turned_im = odd_re[k] * sine + odd_im[k] * cosine
        out_re[k], out_im[k] = even_re[k] + turned_re, even_im[k] + turned_im
        out_re[k + half] = even_re[k] - turned_re
        out_im[k + half] = even_im[k] - turned_im
    return out_re, out_im


def modal_kernel(
    nsec, ndof, steps,
    loads_ref, modes_ref, resp_ref, pattern_ref, dev_ref, eigen_ref, loss_ref, omega_ref,
    mine_ref, three_ref,
    acc, send_a, recv_a, send_b, recv_b, coef, own, near, sa, ra, sb, rb, sc, rc,
):
    step = pl.program_id(0)
    sec, dof = lax.axis_index("sector"), lax.axis_index("dof")
    count = nsec * ndof
    me = sec * ndof + dof
    rows, modes_all = acc.shape
    freqs, half = rows // 2, modes_all // ndof
    groups, share = half // LANES, freqs // nsec
    part = groups * share
    barrier = pltpu.get_barrier_semaphore()

    def peer(k):
        return lax.rem(me + k, count)

    def place(device):
        return {"sector": device // ndof, "dof": lax.rem(device, ndof)}

    @pl.when(step == 0)
    def _():
        acc[...] = jnp.zeros_like(acc)

        def greet(k, carry):
            pl.semaphore_signal(barrier, inc=1, device_id=place(peer(k)), device_id_type=MESH)
            return carry

        lax.fori_loop(1, count, greet, 0)

    acc[...] += jnp.dot(loads_ref[...], modes_ref[...], preferred_element_type=jnp.float32)

    def pick(values):
        total = None
        for d in range(ndof):
            term = jnp.where(dof == d, values[:, d * half : (d + 1) * half], 0.0)
            total = term if total is None else total + term
        return total

    def pieces():
        for kind in range(2):
            for g in range(groups):
                yield kind, g, (kind * groups + g) * share

    @pl.when(step == steps - 1)
    def _():
        table = dev_ref[...]
        chosen = lax.broadcasted_iota(jnp.int32, table.shape, 0) == pattern_ref[0]
        dev_row = pick(jnp.sum(jnp.where(chosen, table, 0.0), axis=0, keepdims=True))
        scaled = dev_row * resp_ref[...]
        for d in range(ndof):
            cols = slice(d * half, (d + 1) * half)
            acc[:, cols] = acc[:, cols] - jnp.where(dof == d, scaled, 0.0)
        for t in range(nsec):
            for d in range(ndof):
                parts = []
                for kind, g, _ in pieces():
                    first = kind * freqs + t * share
                    left = d * half + g * LANES
                    parts.append(acc[first : first + share, left : left + LANES])
                send_a[t * ndof + d] = jnp.concatenate(parts, 0).astype(jnp.bfloat16)
        pl.semaphore_wait(barrier, count - 1)

        def copy_a(to, origin):
            return pltpu.make_async_remote_copy(
                src_ref=send_a.at[to], dst_ref=recv_a.at[origin],
                send_sem=sa.at[to], recv_sem=ra.at[origin],
                device_id=place(to), device_id_type=MESH,
            )

        def copy_b(to, origin):
            return pltpu.make_async_remote_copy(
                src_ref=send_b.at[to // ndof], dst_ref=recv_b.at[origin],
                send_sem=sb.at[to], recv_sem=rb.at[origin],
                device_id=place(to), device_id_type=MESH,
            )

        def start_a(k, carry):
            copy_a(peer(k), me).start()
            return carry

        lax.fori_loop(1, count, start_a, 0)
        recv_a[pl.ds(me, 1)] = send_a[pl.ds(me, 1)]

        row = lax.rem(lax.broadcasted_iota(jnp.int32, (part, LANES), 0), share)
        omega = jnp.zeros((part, LANES), jnp.float32)
        for j in range(share):
            omega = jnp.where(row == j, omega_ref[sec * share + j], omega)

        def spread(line):
            line = pick(line)
            return jnp.concatenate(
                [
                    jnp.broadcast_to(line[:, g * LANES : (g + 1) * LANES], (share, LANES))
                    for g in range(groups)
                ],
                0,
            )

        loss = spread(loss_ref[...])
        for h in range(nsec):
            stiff = spread(eigen_ref[h : h + 1, :])
            shifted, damped = stiff - omega, loss * stiff
            denom = shifted * shifted + damped * damped
            coef[0, h] = shifted / denom
            coef[1, h] = damped / denom

        def wait_a(k, carry):
            copy_a(peer(k), peer(k)).wait_recv()
            return carry

        lax.fori_loop(1, count, wait_a, 0)
        rest_re, rest_im = [], []
        for s in range(nsec):
            block = recv_a[s * ndof].astype(jnp.float32)
            for d in range(1, ndof):
                block = block + recv_a[s * ndof + d].astype(jnp.float32)
            rest_re.append(block[:part])
            rest_im.append(block[part:])
        spec_re, spec_im = transform(rest_re, rest_im, -1.0)
        solved_re, solved_im = [], []
        for h in range(nsec):
            a, b = coef[0, h], coef[1, h]
            solved_re.append(spec_re[h] * a + spec_im[h] * b)
            solved_im.append(spec_im[h] * a - spec_re[h] * b)
        out_re, out_im = transform(solved_re, solved_im, 1.0)
        for s in range(nsec):
            block = jnp.concatenate([out_re[s], out_im[s]], 0) * (1.0 / nsec)
            send_b[s] = block.astype(jnp.bfloat16)

        def start_b(k, carry):
            copy_b(peer(k), me).start()
            return carry

        lax.fori_loop(1, count, start_b, 0)
        recv_b[pl.ds(me, 1)] = send_b[pl.ds(sec, 1)]

        def wait_b(k, carry):
            copy_b(peer(k), peer(k)).wait_recv()
            return carry

        lax.fori_loop(1, count, wait_b, 0)
        for t in range(nsec):
            for d in range(ndof):
                block = recv_b[t * ndof + d].astype(jnp.float32)
                for kind, g, at in pieces():
                    first = kind * freqs + t * share
                    left = d * half + g * LANES
                    acc[first : first + share, left : left + LANES] = block[at : at + share]
        own[...] = acc[...].astype(jnp.bfloat16)

        def copy_c(side):
            to = lax.rem(sec + (nsec - 1, 1)[side], nsec)
            return pltpu.make_async_remote_copy(
                src_ref=own, dst_ref=near.at[side],
                send_sem=sc.at[side], recv_sem=rc.at[side],
                device_id={"sector": to, "dof": dof}, device_id_type=MESH,
            )

        for side in range(2):
            copy_c(side).start()
        mine_ref[...] = pick(acc[...])
        three_ref[:rows] = own[...]

        def sent(k, carry):
            copy_a(peer(k), me).wait_send()
            copy_b(peer(k), me).wait_send()
            return carry

        lax.fori_loop(1, count, sent, 0)
        for side in range(2):
            copy_c(side).wait()
            three_ref[(side + 1) * rows : (side + 2) * rows] = near[side]


def modal_solve(loads, modes, response, pattern, deviation, eigen, loss, omega_sq):
    rows, depth = loads.shape
    modes_all = modes.shape[1]
    nsec, ndof = lax.axis_size("sector"), lax.axis_size("dof")
    half = modes_all // ndof
    count = nsec * ndof
    part = (half // LANES) * (rows // 2 // nsec)
    tile = min(depth, 2048)
    steps = depth // tile

    def still(shape):
        return pl.BlockSpec(shape, lambda k: (0,) * len(shape))

    smem = pl.BlockSpec(memory_space=pltpu.SMEM)
    block = (2 * part, LANES)
    return pl.pallas_call(
        functools.partial(modal_kernel, nsec, ndof, steps),
        grid=(steps,),
        out_shape=(
            jax.ShapeDtypeStruct((rows, half), jnp.float32),
            jax.ShapeDtypeStruct((3 * rows, modes_all), jnp.bfloat16),
        ),
        in_specs=[
            pl.BlockSpec((rows, tile), lambda k: (0, k)),
            pl.BlockSpec((tile, modes_all), lambda k: (k, 0)),
            still(response.shape),
            smem,
            still(deviation.shape),
            still(eigen.shape),
            still((1, modes_all)),
            smem,
        ],
        out_specs=(still((rows, half)), still((3 * rows, modes_all))),
        scratch_shapes=[
            pltpu.VMEM((rows, modes_all), jnp.float32),
            pltpu.VMEM((count,) + block, jnp.bfloat16),
            pltpu.VMEM((count,) + block, jnp.bfloat16),
            pltpu.VMEM((nsec,) + block, jnp.bfloat16),
            pltpu.VMEM((count,) + block, jnp.bfloat16),
            pltpu.VMEM((2, nsec, part, LANES), jnp.float32),
            pltpu.VMEM((rows, modes_all), jnp.bfloat16),
            pltpu.VMEM((2, rows, modes_all), jnp.bfloat16),
            pltpu.SemaphoreType.DMA((count,)),
            pltpu.SemaphoreType.DMA((count,)),
            pltpu.SemaphoreType.DMA((count,)),
            pltpu.SemaphoreType.DMA((count,)),
            pltpu.SemaphoreType.DMA((2,)),
            pltpu.SemaphoreType.DMA((2,)),
        ],
        compiler_params=pltpu.CompilerParams(
            dimension_semantics=("arbitrary",), collective_id=0, has_side_effects=True
        ),
        name="modal_solve",
    )(loads, modes, response, pattern, deviation, eigen, loss.reshape(1, modes_all), omega_sq)


def recover_kernel(
    steps, three_ref, modes_ref, left_ref, right_ref, out_ref, here, after, before
):
    step = pl.program_id(0)
    rows = out_ref.shape[0]
    tile, wide = modes_ref.shape[0], out_ref.shape[1]
    contract = (((1,), (1,)), ((), ()))

    @pl.when(step < steps)
    def _():
        found = lax.dot_general(
            modes_ref[...], three_ref[...], contract, preferred_element_type=jnp.float32
        )
        span = pl.ds(pl.multiple_of(step * tile, tile), tile)
        here[span, :] = found[:, :rows]
        after[span, :] = found[:, rows : 2 * rows]
        before[span, :] = found[:, 2 * rows :]

    @pl.when(step == steps - 1)
    def _():
        entries = left_ref.shape[0]
        group = math.gcd(entries, 8)

        def blend(block, carry):
            new = []
            for j in range(group):
                left, right = left_ref[block * group + j], right_ref[block * group + j]
                new.append((right, here[pl.ds(right, 1), :] + after[pl.ds(left, 1), :]))
                new.append((left, before[pl.ds(right, 1), :] + here[pl.ds(left, 1), :]))
            for at, value in new:
                here[pl.ds(at, 1), :] = 0.5 * value
            return carry

        lax.fori_loop(0, entries // group, blend, 0)

    @pl.when(step >= steps)
    def _():
        span = pl.ds(pl.multiple_of((step - steps) * wide, wide), wide)
        shape = (rows, rows)
        same = lax.broadcasted_iota(jnp.int32, shape, 0) == lax.broadcasted_iota(
            jnp.int32, shape, 1
        )
        eye = jnp.where(same, 1.0, 0.0).astype(jnp.bfloat16)
        out_ref[...] = lax.dot_general(
            eye, here[span, :].astype(jnp.bfloat16), contract, preferred_element_type=jnp.float32
        ).astype(jnp.bfloat16)


def recover(three, modes, left, right):
    depth, modes_all = modes.shape
    rows = three.shape[0] // 3
    tile, wide = min(depth, 1024), min(depth, 2048)
    steps = depth // tile
    smem = pl.BlockSpec(memory_space=pltpu.SMEM)
    return pl.pallas_call(
        functools.partial(recover_kernel, steps),
        grid=(steps + depth // wide,),
        out_shape=jax.ShapeDtypeStruct((rows, depth), jnp.bfloat16),
        in_specs=[
            pl.BlockSpec(three.shape, lambda k: (0, 0)),
            pl.BlockSpec((tile, modes_all), lambda k: (jnp.minimum(k, steps - 1), 0)),
            smem,
            smem,
        ],
        out_specs=pl.BlockSpec((rows, wide), lambda k: (0, jnp.maximum(k - steps, 0))),
        scratch_shapes=[pltpu.VMEM((depth, rows), jnp.float32)] * 3,
        compiler_params=pltpu.CompilerParams(
            dimension_semantics=("arbitrary",), vmem_limit_bytes=60 * 1024 * 1024
        ),
        name="recover",
    )(three, modes, left, right)


def shards(
    loads, modes, response, pattern, deviation, eigen, loss, omega_sq, iface_left, iface_right
):
    mine, three = modal_solve(
        loads[0], modes, response[0], pattern, deviation, eigen, loss, omega_sq
    )
    return mine[None], recover(three, modes, iface_left, iface_right)[None]


def solution(mesh):
    placed = (
        P("sector", None, "dof"),
        P("dof", None),
        P("sector", None, "dof"),
        P("sector"),
        P(),
        P(),
        P(),
        P(),
        P("dof"),
        P("dof"),
    )
    return jax.shard_map(
        shards,
        mesh=mesh,
        in_specs=placed,
        out_specs=(P("sector", None, "dof"), P("sector", None, "dof")),
        check_vma=False,
    )
```

```python
import functools
import math

import jax
import jax.numpy as jnp
from jax import lax
from jax.experimental import pallas as pl
from jax.experimental.pallas import tpu as pltpu
from jax.sharding import PartitionSpec as P

MESH = pl.DeviceIdType.MESH
LANES = 128
LIMIT = 50 * 1024 * 1024


def transform(re, im, sign):
    n = len(re)
    if n == 1:
        return re, im
    if n % 2:
        out_re, out_im = [], []
        for h in range(n):
            sum_re, sum_im = re[0], im[0]
            for s in range(1, n):
                turn = 2.0 * math.pi * ((h * s) % n) / n
                cosine, sine = math.cos(turn), sign * math.sin(turn)
                sum_re = sum_re + re[s] * cosine - im[s] * sine
                sum_im = sum_im + im[s] * cosine + re[s] * sine
            out_re.append(sum_re)
            out_im.append(sum_im)
        return out_re, out_im
    even_re, even_im = transform(re[0::2], im[0::2], sign)
    odd_re, odd_im = transform(re[1::2], im[1::2], sign)
    half = n // 2
    out_re, out_im = [None] * n, [None] * n
    for k in range(half):
        if k == 0:
            turned_re, turned_im = odd_re[k], odd_im[k]
        elif 4 * k == n:
            turned_re, turned_im = -sign * odd_im[k], sign * odd_re[k]
        else:
            cosine = math.cos(2.0 * math.pi * k / n)
            sine = sign * math.sin(2.0 * math.pi * k / n)
            turned_re = odd_re[k] * cosine - odd_im[k] * sine
            turned_im = odd_re[k] * sine + odd_im[k] * cosine
        out_re[k], out_im[k] = even_re[k] + turned_re, even_im[k] + turned_im
        out_re[k + half] = even_re[k] - turned_re
        out_im[k + half] = even_im[k] - turned_im
    return out_re, out_im


def modal_kernel(
    nsec, ndof, steps,
    loads_ref, modes_ref, resp_ref, pattern_ref, dev_ref, eigen_ref, loss_ref, omega_ref,
    left_ref, right_ref, mine_ref, here_ref, new_ref,
    acc, held, kept_ref, after, before, send_a, recv_a, send_b, recv_b, coef, own, near,
    sl, sm, sa, ra, sb, rb, sc, rc,
):
    sec, dof = lax.axis_index("sector"), lax.axis_index("dof")
    count = nsec * ndof
    me = sec * ndof + dof
    rows, modes_all = acc.shape
    freqs, half = rows // 2, modes_all // ndof
    groups, share = half // LANES, freqs // nsec
    part = groups * share
    barrier = pltpu.get_barrier_semaphore()

    def peer(k):
        return lax.rem(me + k, count)

    def place(device):
        return {"sector": device // ndof, "dof": lax.rem(device, ndof)}

    tile = modes_ref.shape[0] // steps

    def fetch(c):
        span = pl.ds(pl.multiple_of(c * tile, tile), tile)
        return (
            pltpu.make_async_copy(loads_ref.at[:, span], held.at[:, span], sl.at[c]),
            pltpu.make_async_copy(modes_ref.at[span, :], kept_ref.at[span, :], sm.at[c]),
        )

    def begin(c, carry):
        for copy in fetch(c):
            copy.start()
        return carry

    lax.fori_loop(0, steps, begin, 0)
    acc[...] = jnp.zeros_like(acc)

    def greet(k, carry):
        pl.semaphore_signal(barrier, inc=1, device_id=place(peer(k)), device_id_type=MESH)
        return carry

    lax.fori_loop(1, count, greet, 0)

    def pick(values):
        total = None
        for d in range(ndof):
            term = jnp.where(dof == d, values[:, d * half : (d + 1) * half], 0.0)
            total = term if total is None else total + term
        return total

    def pieces():
        for kind in range(2):
            for g in range(groups):
                yield kind, g, (kind * groups + g) * share

    table = dev_ref[...]
    chosen = lax.broadcasted_iota(jnp.int32, table.shape, 0) == pattern_ref[0]
    dev_row = pick(jnp.sum(jnp.where(chosen, table, 0.0), axis=0, keepdims=True))
    scaled = dev_row * resp_ref[...]
    row = lax.rem(lax.broadcasted_iota(jnp.int32, (part, LANES), 0), share)
    omega = jnp.zeros((part, LANES), jnp.float32)
    for j in range(share):
        omega = jnp.where(row == j, omega_ref[sec * share + j], omega)

    def spread(line):
        line = pick(line)
        return jnp.concatenate(
            [
                jnp.broadcast_to(line[:, g * LANES : (g + 1) * LANES], (share, LANES))
                for g in range(groups)
            ],
            0,
        )

    loss = spread(loss_ref[...])
    for h in range(nsec):
        stiff = spread(eigen_ref[h : h + 1, :])
        shifted, damped = stiff - omega, loss * stiff
        denom = shifted * shifted + damped * damped
        coef[0, h] = shifted / denom
        coef[1, h] = damped / denom

    def multiply(c, carry):
        for copy in fetch(c):
            copy.wait()
        span = pl.ds(pl.multiple_of(c * tile, tile), tile)
        acc[...] += jnp.dot(held[:, span], kept_ref[span, :], preferred_element_type=jnp.float32)
        return carry

    lax.fori_loop(0, steps, multiply, 0)
    for d in range(ndof):
        cols = slice(d * half, (d + 1) * half)
        acc[:, cols] = acc[:, cols] - jnp.where(dof == d, scaled, 0.0)
    for t in range(nsec):
        for d in range(ndof):
            parts = []
            for kind, g, _ in pieces():
                first = kind * freqs + t * share
                left = d * half + g * LANES
                parts.append(acc[first : first + share, left : left + LANES])
            send_a[t * ndof + d] = jnp.concatenate(parts, 0).astype(jnp.bfloat16)
    pl.semaphore_wait(barrier, count - 1)

    def copy_a(to, origin):
        return pltpu.make_async_remote_copy(
            src_ref=send_a.at[to], dst_ref=recv_a.at[origin],
            send_sem=sa.at[to], recv_sem=ra.at[origin],
            device_id=place(to), device_id_type=MESH,
        )

    def copy_b(to, origin):
        return pltpu.make_async_remote_copy(
            src_ref=send_b.at[to // ndof], dst_ref=recv_b.at[origin],
            send_sem=sb.at[to], recv_sem=rb.at[origin],
            device_id=place(to), device_id_type=MESH,
        )

    def start_a(k, carry):
        copy_a(peer(k), me).start()
        return carry

    lax.fori_loop(1, count, start_a, 0)
    recv_a[pl.ds(me, 1)] = send_a[pl.ds(me, 1)]

    def wait_a(k, carry):
        copy_a(peer(k), peer(k)).wait_recv()
        return carry

    lax.fori_loop(1, count, wait_a, 0)
    rest_re, rest_im = [], []
    for s in range(nsec):
        block = recv_a[s * ndof].astype(jnp.float32)
        for d in range(1, ndof):
            block = block + recv_a[s * ndof + d].astype(jnp.float32)
        rest_re.append(block[:part])
        rest_im.append(block[part:])
    spec_re, spec_im = transform(rest_re, rest_im, -1.0)
    solved_re, solved_im = [], []
    for h in range(nsec):
        a, b = coef[0, h], coef[1, h]
        solved_re.append(spec_re[h] * a + spec_im[h] * b)
        solved_im.append(spec_im[h] * a - spec_re[h] * b)
    out_re, out_im = transform(solved_re, solved_im, 1.0)
    for s in range(nsec):
        block = jnp.concatenate([out_re[s], out_im[s]], 0) * (1.0 / nsec)
        send_b[s] = block.astype(jnp.bfloat16)

    def start_b(k, carry):
        copy_b(peer(k), me).start()
        return carry

    lax.fori_loop(1, count, start_b, 0)
    recv_b[pl.ds(me, 1)] = send_b[pl.ds(sec, 1)]

    def wait_b(k, carry):
        copy_b(peer(k), peer(k)).wait_recv()
        return carry

    lax.fori_loop(1, count, wait_b, 0)
    for t in range(nsec):
        for d in range(ndof):
            block = recv_b[t * ndof + d].astype(jnp.float32)
            for kind, g, at in pieces():
                first = kind * freqs + t * share
                left = d * half + g * LANES
                acc[first : first + share, left : left + LANES] = block[at : at + share]
    own[...] = acc[...].astype(jnp.bfloat16)

    def copy_c(side):
        to = lax.rem(sec + (nsec - 1, 1)[side], nsec)
        return pltpu.make_async_remote_copy(
            src_ref=own, dst_ref=near.at[side],
            send_sem=sc.at[side], recv_sem=rc.at[side],
            device_id={"sector": to, "dof": dof}, device_id_type=MESH,
        )

    for side in range(2):
        copy_c(side).start()
    mine_ref[...] = pick(acc[...])
    contract = (((1,), (1,)), ((), ()))

    def project(c, carry):
        span = pl.ds(pl.multiple_of(c * tile, tile), tile)
        here_ref[span, :] = lax.dot_general(
            kept_ref[span, :], own[...], contract, preferred_element_type=jnp.float32
        )
        return carry

    lax.fori_loop(0, steps, project, 0)

    def sent(k, carry):
        copy_a(peer(k), me).wait_send()
        copy_b(peer(k), me).wait_send()
        return carry

    lax.fori_loop(1, count, sent, 0)
    for side in range(2):
        copy_c(side).wait()

    def project_near(c, carry):
        span = pl.ds(pl.multiple_of(c * tile, tile), tile)
        for side, target in ((0, after), (1, before)):
            target[span, :] = lax.dot_general(
                kept_ref[span, :], near[side], contract, preferred_element_type=jnp.float32
            )
        return carry

    lax.fori_loop(0, steps, project_near, 0)
    entries = left_ref.shape[0]
    group = math.gcd(entries, 8)

    def blend(block, carry):
        for j in range(group):
            at = block * group + j
            left, right = left_ref[at], right_ref[at]
            left_new = before[pl.ds(right, 1), :] + here_ref[pl.ds(left, 1), :]
            right_new = here_ref[pl.ds(right, 1), :] + after[pl.ds(left, 1), :]
            new_ref[0, pl.ds(at, 1), :] = 0.5 * left_new
            new_ref[1, pl.ds(at, 1), :] = 0.5 * right_new
        return carry

    lax.fori_loop(0, entries // group, blend, 0)


def modal_solve(
    loads, modes, response, pattern, deviation, eigen, loss, omega_sq, left, right
):
    rows, depth = loads.shape
    modes_all = modes.shape[1]
    nsec, ndof = lax.axis_size("sector"), lax.axis_size("dof")
    half = modes_all // ndof
    count = nsec * ndof
    part = (half // LANES) * (rows // 2 // nsec)
    tile = math.gcd(depth, 1024)
    steps = depth // tile
    smem = pl.BlockSpec(memory_space=pltpu.SMEM)
    vmem = pl.BlockSpec(memory_space=pltpu.VMEM)
    away = pl.BlockSpec(memory_space=pltpu.HBM)
    block = (2 * part, LANES)
    return pl.pallas_call(
        functools.partial(modal_kernel, nsec, ndof, steps),
        out_shape=(
            jax.ShapeDtypeStruct((rows, half), jnp.float32),
            pltpu.VMEM((depth, rows), jnp.float32),
            pltpu.VMEM((2, left.shape[0], rows), jnp.float32),
        ),
        in_specs=[away, away, vmem, smem, vmem, vmem, vmem, smem, smem, smem],
        out_specs=(vmem,) * 3,
        scratch_shapes=[
            pltpu.VMEM((rows, modes_all), jnp.float32),
            pltpu.VMEM((rows, depth), jnp.bfloat16),
            pltpu.VMEM((depth, modes_all), jnp.bfloat16),
            pltpu.VMEM((depth, rows), jnp.float32),
            pltpu.VMEM((depth, rows), jnp.float32),
            pltpu.VMEM((count,) + block, jnp.bfloat16),
            pltpu.VMEM((count,) + block, jnp.bfloat16),
            pltpu.VMEM((nsec,) + block, jnp.bfloat16),
            pltpu.VMEM((count,) + block, jnp.bfloat16),
            pltpu.VMEM((2, nsec, part, LANES), jnp.float32),
            pltpu.VMEM((rows, modes_all), jnp.bfloat16),
            pltpu.VMEM((2, rows, modes_all), jnp.bfloat16),
            pltpu.SemaphoreType.DMA((steps,)),
            pltpu.SemaphoreType.DMA((steps,)),
            pltpu.SemaphoreType.DMA((count,)),
            pltpu.SemaphoreType.DMA((count,)),
            pltpu.SemaphoreType.DMA((count,)),
            pltpu.SemaphoreType.DMA((count,)),
            pltpu.SemaphoreType.DMA((2,)),
            pltpu.SemaphoreType.DMA((2,)),
        ],
        compiler_params=pltpu.CompilerParams(
            collective_id=0, has_side_effects=True, vmem_limit_bytes=LIMIT
        ),
        name="modal_solve",
    )(
        loads, modes, response, pattern, deviation, eigen, loss.reshape(1, modes_all), omega_sq,
        left, right,
    )


def recover_kernel(wide, here_in, new_ref, left_ref, right_ref, out_ref, here, buffer, sems):
    rows, depth = out_ref.shape
    contract = (((1,), (1,)), ((), ()))
    entries = left_ref.shape[0]
    group = math.gcd(entries, 8)

    def place(block, carry):
        for j in range(group):
            at = block * group + j
            here[pl.ds(left_ref[at], 1), :] = new_ref[0, pl.ds(at, 1), :]
            here[pl.ds(right_ref[at], 1), :] = new_ref[1, pl.ds(at, 1), :]
        return carry

    lax.fori_loop(0, entries // group, place, 0)
    shape = (rows, rows)
    same = lax.broadcasted_iota(jnp.int32, shape, 0) == lax.broadcasted_iota(jnp.int32, shape, 1)
    eye = jnp.where(same, 1.0, 0.0).astype(jnp.bfloat16)
    pieces = depth // wide

    def store(c):
        return pltpu.make_async_copy(
            buffer.at[c], out_ref.at[:, pl.ds(c * wide, wide)], sems.at[c]
        )

    for c in range(pieces):
        buffer[c] = lax.dot_general(
            eye,
            here[c * wide : (c + 1) * wide, :].astype(jnp.bfloat16),
            contract,
            preferred_element_type=jnp.float32,
        ).astype(jnp.bfloat16)
        store(c).start()
    for c in range(pieces):
        store(c).wait()


def recover(here, new, left, right):
    depth, rows = here.shape
    wide = math.gcd(depth, 2048)
    smem = pl.BlockSpec(memory_space=pltpu.SMEM)
    vmem = pl.BlockSpec(memory_space=pltpu.VMEM)
    return pl.pallas_call(
        functools.partial(recover_kernel, wide),
        out_shape=(
            jax.ShapeDtypeStruct((rows, depth), jnp.bfloat16),
            pltpu.VMEM((depth, rows), jnp.float32),
        ),
        in_specs=[vmem, vmem, smem, smem],
        out_specs=(pl.BlockSpec(memory_space=pl.ANY), vmem),
        input_output_aliases={0: 1},
        scratch_shapes=[
            pltpu.VMEM((depth // wide, rows, wide), jnp.bfloat16),
            pltpu.SemaphoreType.DMA((depth // wide,)),
        ],
        compiler_params=pltpu.CompilerParams(vmem_limit_bytes=LIMIT),
        name="recover",
    )(here, new, left, right)[0]


def shards(
    loads, modes, response, pattern, deviation, eigen, loss, omega_sq, iface_left, iface_right
):
    mine, here, new = modal_solve(
        loads[0], modes, response[0], pattern, deviation, eigen, loss, omega_sq,
        iface_left, iface_right,
    )
    return mine[None], recover(here, new, iface_left, iface_right)[None]


def solution(mesh):
    placed = (
        P("sector", None, "dof"),
        P("dof", None),
        P("sector", None, "dof"),
        P("sector"),
        P(),
        P(),
        P(),
        P(),
        P("dof"),
        P("dof"),
    )
    return jax.shard_map(
        shards,
        mesh=mesh,
        in_specs=placed,
        out_specs=(P("sector", None, "dof"), P("sector", None, "dof")),
        check_vma=False,
    )
```

```python
import functools
import math

import jax
import jax.numpy as jnp
from jax import lax
from jax.experimental import pallas as pl
from jax.experimental.pallas import tpu as pltpu
from jax.sharding import PartitionSpec as P

MESH = pl.DeviceIdType.MESH
LANES = 128
LIMIT = 50 * 1024 * 1024


def transform(re, im, sign):
    n = len(re)
    if n == 1:
        return re, im
    if n % 2:
        out_re, out_im = [], []
        for h in range(n):
            sum_re, sum_im = re[0], im[0]
            for s in range(1, n):
                turn = 2.0 * math.pi * ((h * s) % n) / n
                cosine, sine = math.cos(turn), sign * math.sin(turn)
                sum_re = sum_re + re[s] * cosine - im[s] * sine
                sum_im = sum_im + im[s] * cosine + re[s] * sine
            out_re.append(sum_re)
            out_im.append(sum_im)
        return out_re, out_im
    even_re, even_im = transform(re[0::2], im[0::2], sign)
    odd_re, odd_im = transform(re[1::2], im[1::2], sign)
    half = n // 2
    out_re, out_im = [None] * n, [None] * n
    for k in range(half):
        if k == 0:
            turned_re, turned_im = odd_re[k], odd_im[k]
        elif 4 * k == n:
            turned_re, turned_im = -sign * odd_im[k], sign * odd_re[k]
        else:
            cosine = math.cos(2.0 * math.pi * k / n)
            sine = sign * math.sin(2.0 * math.pi * k / n)
            turned_re = odd_re[k] * cosine - odd_im[k] * sine
            turned_im = odd_re[k] * sine + odd_im[k] * cosine
        out_re[k], out_im[k] = even_re[k] + turned_re, even_im[k] + turned_im
        out_re[k + half] = even_re[k] - turned_re
        out_im[k + half] = even_im[k] - turned_im
    return out_re, out_im


def modal_kernel(
    nsec, ndof, steps,
    loads_ref, modes_ref, resp_ref, pattern_ref, dev_ref, eigen_ref, loss_ref, omega_ref,
    left_ref, right_ref, mine_ref, here_ref, new_ref,
    acc, held, kept_ref, after, before, send_a, recv_a, send_b, recv_b, coef, own, near,
    sl, sm, sa, ra, sb, rb, sc, rc,
):
    sec, dof = lax.axis_index("sector"), lax.axis_index("dof")
    count = nsec * ndof
    me = sec * ndof + dof
    rows, modes_all = acc.shape
    freqs, half = rows // 2, modes_all // ndof
    groups, share = half // LANES, freqs // nsec
    part = groups * share
    barrier = pltpu.get_barrier_semaphore()

    def peer(k):
        return lax.rem(me + k, count)

    def place(device):
        return {"sector": device // ndof, "dof": lax.rem(device, ndof)}

    tile = modes_ref.shape[0] // steps

    def fetch(c):
        span = pl.ds(pl.multiple_of(c * tile, tile), tile)
        return (
            pltpu.make_async_copy(loads_ref.at[:, span], held.at[:, span], sl.at[c]),
            pltpu.make_async_copy(modes_ref.at[span, :], kept_ref.at[span, :], sm.at[c]),
        )

    def begin(c, carry):
        for copy in fetch(c):
            copy.start()
        return carry

    lax.fori_loop(0, steps, begin, 0)
    acc[...] = jnp.zeros_like(acc)

    def greet(k, carry):
        pl.semaphore_signal(barrier, inc=1, device_id=place(peer(k)), device_id_type=MESH)
        return carry

    lax.fori_loop(1, count, greet, 0)

    def pick(values):
        total = None
        for d in range(ndof):
            term = jnp.where(dof == d, values[:, d * half : (d + 1) * half], 0.0)
            total = term if total is None else total + term
        return total

    def pieces():
        for kind in range(2):
            for g in range(groups):
                yield kind, g, (kind * groups + g) * share

    table = dev_ref[...]
    chosen = lax.broadcasted_iota(jnp.int32, table.shape, 0) == pattern_ref[0]
    dev_row = pick(jnp.sum(jnp.where(chosen, table, 0.0), axis=0, keepdims=True))
    scaled = dev_row * resp_ref[...]
    row = lax.rem(lax.broadcasted_iota(jnp.int32, (part, LANES), 0), share)
    omega = jnp.zeros((part, LANES), jnp.float32)
    for j in range(share):
        omega = jnp.where(row == j, omega_ref[sec * share + j], omega)

    def spread(line):
        line = pick(line)
        return jnp.concatenate(
            [
                jnp.broadcast_to(line[:, g * LANES : (g + 1) * LANES], (share, LANES))
                for g in range(groups)
            ],
            0,
        )

    loss = spread(loss_ref[...])
    for h in range(nsec):
        stiff = spread(eigen_ref[h : h + 1, :])
        shifted, damped = stiff - omega, loss * stiff
        denom = shifted * shifted + damped * damped
        coef[0, h] = shifted / denom
        coef[1, h] = damped / denom

    def multiply(c, carry):
        for copy in fetch(c):
            copy.wait()
        span = pl.ds(pl.multiple_of(c * tile, tile), tile)
        acc[...] += jnp.dot(held[:, span], kept_ref[span, :], preferred_element_type=jnp.float32)
        return carry

    lax.fori_loop(0, steps, multiply, 0)
    for d in range(ndof):
        cols = slice(d * half, (d + 1) * half)
        acc[:, cols] = acc[:, cols] - jnp.where(dof == d, scaled, 0.0)
    for t in range(nsec):
        for d in range(ndof):
            parts = []
            for kind, g, _ in pieces():
                first = kind * freqs + t * share
                left = d * half + g * LANES
                parts.append(acc[first : first + share, left : left + LANES])
            send_a[t * ndof + d] = jnp.concatenate(parts, 0).astype(jnp.bfloat16)
    pl.semaphore_wait(barrier, count - 1)

    def copy_a(to, origin):
        return pltpu.make_async_remote_copy(
            src_ref=send_a.at[to], dst_ref=recv_a.at[origin],
            send_sem=sa.at[to], recv_sem=ra.at[origin],
            device_id=place(to), device_id_type=MESH,
        )

    def copy_b(to, origin):
        return pltpu.make_async_remote_copy(
            src_ref=send_b.at[to // ndof], dst_ref=recv_b.at[origin],
            send_sem=sb.at[to], recv_sem=rb.at[origin],
            device_id=place(to), device_id_type=MESH,
        )

    def start_a(k, carry):
        copy_a(peer(k), me).start()
        return carry

    lax.fori_loop(1, count, start_a, 0)
    recv_a[pl.ds(me, 1)] = send_a[pl.ds(me, 1)]

    def wait_a(k, carry):
        copy_a(peer(k), peer(k)).wait_recv()
        return carry

    lax.fori_loop(1, count, wait_a, 0)
    rest_re, rest_im = [], []
    for s in range(nsec):
        block = recv_a[s * ndof].astype(jnp.float32)
        for d in range(1, ndof):
            block = block + recv_a[s * ndof + d].astype(jnp.float32)
        rest_re.append(block[:part])
        rest_im.append(block[part:])
    spec_re, spec_im = transform(rest_re, rest_im, -1.0)
    solved_re, solved_im = [], []
    for h in range(nsec):
        a, b = coef[0, h], coef[1, h]
        solved_re.append(spec_re[h] * a + spec_im[h] * b)
        solved_im.append(spec_im[h] * a - spec_re[h] * b)
    out_re, out_im = transform(solved_re, solved_im, 1.0)
    for s in range(nsec):
        block = jnp.concatenate([out_re[s], out_im[s]], 0) * (1.0 / nsec)
        send_b[s] = block.astype(jnp.bfloat16)

    def start_b(k, carry):
        copy_b(peer(k), me).start()
        return carry

    lax.fori_loop(1, count, start_b, 0)
    recv_b[pl.ds(me, 1)] = send_b[pl.ds(sec, 1)]

    def wait_b(k, carry):
        copy_b(peer(k), peer(k)).wait_recv()
        return carry

    lax.fori_loop(1, count, wait_b, 0)
    for t in range(nsec):
        for d in range(ndof):
            block = recv_b[t * ndof + d].astype(jnp.float32)
            for kind, g, at in pieces():
                first = kind * freqs + t * share
                left = d * half + g * LANES
                acc[first : first + share, left : left + LANES] = block[at : at + share]
    own[...] = acc[...].astype(jnp.bfloat16)

    def copy_c(side):
        to = lax.rem(sec + (nsec - 1, 1)[side], nsec)
        return pltpu.make_async_remote_copy(
            src_ref=own, dst_ref=near.at[side],
            send_sem=sc.at[side], recv_sem=rc.at[side],
            device_id={"sector": to, "dof": dof}, device_id_type=MESH,
        )

    for side in range(2):
        copy_c(side).start()
    mine_ref[...] = pick(acc[...])
    contract = (((1,), (1,)), ((), ()))

    def project(c, carry):
        span = pl.ds(pl.multiple_of(c * tile, tile), tile)
        here_ref[span, :] = lax.dot_general(
            kept_ref[span, :], own[...], contract, preferred_element_type=jnp.float32
        )
        return carry

    lax.fori_loop(0, steps, project, 0)

    def sent(k, carry):
        copy_a(peer(k), me).wait_send()
        copy_b(peer(k), me).wait_send()
        return carry

    lax.fori_loop(1, count, sent, 0)
    for side in range(2):
        copy_c(side).wait()

    def project_near(c, carry):
        span = pl.ds(pl.multiple_of(c * tile, tile), tile)
        found = lax.dot_general(
            kept_ref[span, :],
            near[...].reshape(2 * rows, modes_all),
            contract,
            preferred_element_type=jnp.float32,
        )
        after[span, :] = found[:, :rows]
        before[span, :] = found[:, rows:]
        return carry

    lax.fori_loop(0, steps, project_near, 0)
    entries = left_ref.shape[0]
    group = math.gcd(entries, 8)

    def blend(block, carry):
        for j in range(group):
            at = block * group + j
            left, right = left_ref[at], right_ref[at]
            left_new = before[pl.ds(right, 1), :] + here_ref[pl.ds(left, 1), :]
            right_new = here_ref[pl.ds(right, 1), :] + after[pl.ds(left, 1), :]
            new_ref[0, pl.ds(at, 1), :] = 0.5 * left_new
            new_ref[1, pl.ds(at, 1), :] = 0.5 * right_new
        return carry

    lax.fori_loop(0, entries // group, blend, 0)


def modal_solve(
    loads, modes, response, pattern, deviation, eigen, loss, omega_sq, left, right
):
    rows, depth = loads.shape
    modes_all = modes.shape[1]
    nsec, ndof = lax.axis_size("sector"), lax.axis_size("dof")
    half = modes_all // ndof
    count = nsec * ndof
    part = (half // LANES) * (rows // 2 // nsec)
    tile = math.gcd(depth, 1024)
    steps = depth // tile
    smem = pl.BlockSpec(memory_space=pltpu.SMEM)
    vmem = pl.BlockSpec(memory_space=pltpu.VMEM)
    away = pl.BlockSpec(memory_space=pltpu.HBM)
    block = (2 * part, LANES)
    return pl.pallas_call(
        functools.partial(modal_kernel, nsec, ndof, steps),
        out_shape=(
            jax.ShapeDtypeStruct((rows, half), jnp.float32),
            pltpu.VMEM((depth, rows), jnp.float32),
            pltpu.VMEM((2, left.shape[0], rows), jnp.float32),
        ),
        in_specs=[away, away, vmem, smem, vmem, vmem, vmem, smem, smem, smem],
        out_specs=(vmem,) * 3,
        scratch_shapes=[
            pltpu.VMEM((rows, modes_all), jnp.float32),
            pltpu.VMEM((rows, depth), jnp.bfloat16),
            pltpu.VMEM((depth, modes_all), jnp.bfloat16),
            pltpu.VMEM((depth, rows), jnp.float32),
            pltpu.VMEM((depth, rows), jnp.float32),
            pltpu.VMEM((count,) + block, jnp.bfloat16),
            pltpu.VMEM((count,) + block, jnp.bfloat16),
            pltpu.VMEM((nsec,) + block, jnp.bfloat16),
            pltpu.VMEM((count,) + block, jnp.bfloat16),
            pltpu.VMEM((2, nsec, part, LANES), jnp.float32),
            pltpu.VMEM((rows, modes_all), jnp.bfloat16),
            pltpu.VMEM((2, rows, modes_all), jnp.bfloat16),
            pltpu.SemaphoreType.DMA((steps,)),
            pltpu.SemaphoreType.DMA((steps,)),
            pltpu.SemaphoreType.DMA((count,)),
            pltpu.SemaphoreType.DMA((count,)),
            pltpu.SemaphoreType.DMA((count,)),
            pltpu.SemaphoreType.DMA((count,)),
            pltpu.SemaphoreType.DMA((2,)),
            pltpu.SemaphoreType.DMA((2,)),
        ],
        compiler_params=pltpu.CompilerParams(
            collective_id=0, has_side_effects=True, vmem_limit_bytes=LIMIT
        ),
        name="modal_solve",
    )(
        loads, modes, response, pattern, deviation, eigen, loss.reshape(1, modes_all), omega_sq,
        left, right,
    )


def recover_kernel(wide, here_in, new_ref, left_ref, right_ref, out_ref, here, buffer, sems):
    rows, depth = out_ref.shape
    contract = (((1,), (1,)), ((), ()))
    entries = left_ref.shape[0]
    group = math.gcd(entries, 8)

    def place(block, carry):
        for j in range(group):
            at = block * group + j
            here[pl.ds(left_ref[at], 1), :] = new_ref[0, pl.ds(at, 1), :]
            here[pl.ds(right_ref[at], 1), :] = new_ref[1, pl.ds(at, 1), :]
        return carry

    lax.fori_loop(0, entries // group, place, 0)
    shape = (rows, rows)
    same = lax.broadcasted_iota(jnp.int32, shape, 0) == lax.broadcasted_iota(jnp.int32, shape, 1)
    eye = jnp.where(same, 1.0, 0.0).astype(jnp.bfloat16)
    pieces = depth // wide

    def store(c):
        return pltpu.make_async_copy(
            buffer.at[c], out_ref.at[:, pl.ds(c * wide, wide)], sems.at[c]
        )

    for c in range(pieces):
        buffer[c] = lax.dot_general(
            eye,
            here[c * wide : (c + 1) * wide, :].astype(jnp.bfloat16),
            contract,
            preferred_element_type=jnp.float32,
        ).astype(jnp.bfloat16)
        store(c).start()
    for c in range(pieces):
        store(c).wait()


def recover(here, new, left, right):
    depth, rows = here.shape
    wide = math.gcd(depth, 2048)
    smem = pl.BlockSpec(memory_space=pltpu.SMEM)
    vmem = pl.BlockSpec(memory_space=pltpu.VMEM)
    return pl.pallas_call(
        functools.partial(recover_kernel, wide),
        out_shape=(
            jax.ShapeDtypeStruct((rows, depth), jnp.bfloat16),
            pltpu.VMEM((depth, rows), jnp.float32),
        ),
        in_specs=[vmem, vmem, smem, smem],
        out_specs=(pl.BlockSpec(memory_space=pl.ANY), vmem),
        input_output_aliases={0: 1},
        scratch_shapes=[
            pltpu.VMEM((depth // wide, rows, wide), jnp.bfloat16),
            pltpu.SemaphoreType.DMA((depth // wide,)),
        ],
        compiler_params=pltpu.CompilerParams(vmem_limit_bytes=LIMIT),
        name="recover",
    )(here, new, left, right)[0]


def shards(
    loads, modes, response, pattern, deviation, eigen, loss, omega_sq, iface_left, iface_right
):
    mine, here, new = modal_solve(
        loads[0], modes, response[0], pattern, deviation, eigen, loss, omega_sq,
        iface_left, iface_right,
    )
    return mine[None], recover(here, new, iface_left, iface_right)[None]


def solution(mesh):
    placed = (
        P("sector", None, "dof"),
        P("dof", None),
        P("sector", None, "dof"),
        P("sector"),
        P(),
        P(),
        P(),
        P(),
        P("dof"),
        P("dof"),
    )
    return jax.shard_map(
        shards,
        mesh=mesh,
        in_specs=placed,
        out_specs=(P("sector", None, "dof"), P("sector", None, "dof")),
        check_vma=False,
    )
```
